32 devices in a mesh: groups: 2 (over x), weight: 16 (over z, y, core).
Axes of the slice: x: 2, y: 2, z: 4, core: 2. Of those that a mesh axis runs over, the one named last changes fastest.
Arguments:
- hidden: bfloat16 [128, 8192], P(('groups', 'weight')), parts along dimension 0, may hold values from -6 to 6
- norm_gain: float32 [8192], replicated, may hold values from 0.1 to 1.9
- in_weight: bfloat16 [8192, 2, 8192], P(None, None, 'weight'), may hold values from -0.0625 to 0.0625
- conv_weight: float32 [4, 8192], P(None, 'weight'), may hold values from -0.6 to 0.6
- conv_offset: float32 [8192], P('weight'), may hold values from -0.5 to 0.5
- coef_weight: bfloat16 [8192, 544], P('weight'), may hold values from -0.0625 to 0.0625
- step_weight: bfloat16 [512, 8192], P(None, 'weight'), may hold values from -0.25 to 0.25
- step_bias: float32 [8192], P('weight'), may hold values from -3 to 0.5
- log_rates: float32 [16, 8192], P(None, 'weight'), may hold values from 0 to 2.77
- skip_gain: float32 [8192], P('weight'), may hold values from 0.5 to 1.5
- out_weight: bfloat16 [8192, 8192], P('weight'), may hold values from -0.0625 to 0.0625
- ssm_state: bfloat16 [128, 16, 8192], P('groups', None, 'weight'), parts along dimension 0, may hold values from -6 to 6
- conv_state: bfloat16 [128, 3, 8192], P('groups', None, 'weight'), parts along dimension 0, may hold values from -6 to 6
- live_counts: int32 [32], P('groups'), parts along dimension 0, may hold values from 1 to 3, as said below
Outputs:
- mixed: bfloat16 [128, 8192], P(('groups', 'weight')), parts along dimension 0
- new_state: bfloat16 [128, 16, 8192], P('groups', None, 'weight'), parts along dimension 0
- new_conv: bfloat16 [128, 3, 8192], P('groups', None, 'weight'), parts along dimension 0
The draws below stay inside these ranges and needn't reach their ends.
There are 2 independent parts, one for each index of `groups`. The reference program is written for one: setup_inputs(seed, part) draws one part's arguments, and reference() takes and returns one part's arrays. A program takes and returns all parts, laid end to end along the dimension named above; an argument that names none is the same for every part. Nothing has to cross between parts.
Inputs may be any that keep to these rules, and one draw needn't show every extreme that they name: The live rows of a microbatch are its first live_counts rows; the most, 3, is reached by some microbatch.
All inputs are finite; a program needn't handle non-finite values.
Results may differ from the reference program's by a relative error of at most 0.0039.
Values may be sent and summed in bfloat16 or wider, within the bound.
A program may use at most 64 MiB of HBM per device.

```python
import jax
import jax.numpy as jnp
from jax import lax

D = 8192
E = 8192
NSTATE = 16
DTR = 512
ROWS_DEV = 4
LIVE_MAX = 3
MICRO = 16
R = 64


def draw_live_counts(key, part):
    base = jax.random.fold_in(key, 11)
    first_key, second_key = jax.random.split(base)
    counts = jax.random.randint(first_key, (MICRO,), 1, LIVE_MAX + 1)
    chosen = jax.random.randint(second_key, (), 0, MICRO)
    filled = jnp.where(jnp.arange(MICRO) == chosen, LIVE_MAX, counts)
    return filled.astype(jnp.int32)


def block_scale(stream_key, dims, cuts, least, high):
    factor_of, own = 1.0, jax.random.fold_in(stream_key, 6)
    for axis_at, parts in cuts:
        draws = jnp.exp(jax.random.uniform(jax.random.fold_in(own, axis_at), (parts,), jnp.float32, least / len(cuts), high / len(cuts)))
        factor_of = factor_of * jnp.repeat(draws, dims[axis_at] // parts).reshape([-1 if axis == axis_at else 1 for axis in range(len(dims))])
    return factor_of


def centred(rng, shape, scale, limit, cuts=(), kind=jnp.bfloat16):
    result = scale * jax.random.normal(rng, shape, jnp.float32)
    if cuts:
        result = result * block_scale(rng, shape, cuts, -0.22, 0.18)
    return jnp.clip(result, -limit, limit).astype(kind)


def setup_inputs(seed: int = 0, part: int = 0) -> dict:
    arg_keys = jax.random.split(jax.random.key(seed), 15)
    part_keys = jax.random.split(jax.random.fold_in(arg_keys[14], part), 15)
    hidden = centred(part_keys[0], (R, D), 1.0, 6.0, ((0, 16),))
    norm_gain = jnp.clip(1.0 + 0.18 * jax.random.normal(arg_keys[1], (D,), jnp.float32), 0.1, 1.9)
    in_weight = centred(arg_keys[2], (D, 2, E), D ** -0.5, 0.0625, ((2, 16),))
    conv_weight = jnp.clip(jax.random.uniform(arg_keys[3], (4, E), jnp.float32, -0.6, 0.6) * block_scale(arg_keys[3], (4, E), ((1, 16),), -0.4, 0.0), -0.6, 0.6)
    conv_offset = jnp.clip(jax.random.uniform(arg_keys[4], (E,), jnp.float32, -0.5, 0.5) * block_scale(arg_keys[4], (E,), ((0, 16),), -0.4, 0.0), -0.5, 0.5)
    coef_weight = centred(arg_keys[5], (E, DTR + 2 * NSTATE), E ** -0.5, 0.0625, ((0, 16),))
    step_weight = centred(arg_keys[6], (DTR, E), DTR ** -0.5, 0.25, ((1, 16),))
    step_bias = jnp.clip(-3.0 + 3.5 * jax.random.uniform(arg_keys[7], (E,), jnp.float32) ** block_scale(arg_keys[7], (E,), ((0, 16),), -0.2, 0.2), -3.0, 0.5)
    log_rates = jnp.clip(2.77 * jax.random.uniform(arg_keys[8], (NSTATE, E), jnp.float32) ** block_scale(arg_keys[8], (NSTATE, E), ((1, 16),), -0.2, 0.2), 0.0, 2.77)
    skip_gain = jnp.clip(0.5 + 1.0 * jax.random.uniform(arg_keys[9], (E,), jnp.float32) ** block_scale(arg_keys[9], (E,), ((0, 16),), -0.2, 0.2), 0.5, 1.5)
    out_weight = centred(arg_keys[10], (E, D), E ** -0.5, 0.0625, ((0, 16),))
    ssm_state = centred(part_keys[11], (R, NSTATE, E), 1.0, 6.0, ((2, 16),))
    conv_state = centred(part_keys[12], (R, 3, E), 1.0, 6.0, ((2, 16),))
    live_counts = draw_live_counts(jax.random.fold_in(jax.random.fold_in(arg_keys[14], part), 71), part)
    return {"hidden": hidden, "norm_gain": norm_gain, "in_weight": in_weight, "conv_weight": conv_weight, "conv_offset": conv_offset, "coef_weight": coef_weight, "step_weight": step_weight, "step_bias": step_bias, "log_rates": log_rates, "skip_gain": skip_gain, "out_weight": out_weight, "ssm_state": ssm_state, "conv_state": conv_state, "live_counts": live_counts}


def rms_normed(hidden, norm_gain):
    wide = hidden.astype(jnp.float32)
    factor = lax.rsqrt(lax.optimization_barrier(jnp.mean(wide * wide, axis=-1, keepdims=True)) + 1e-05)
    return (wide * factor * norm_gain).astype(jnp.bfloat16)

def reference(hidden, norm_gain, in_weight, conv_weight, conv_offset, coef_weight, step_weight, step_bias, log_rates, skip_gain, out_weight, ssm_state, conv_state, live_counts):
    total_rows = hidden.shape[0]
    row_ids = jnp.arange(total_rows, dtype=jnp.int32)
    per_row = jnp.repeat(live_counts, ROWS_DEV, total_repeat_length=total_rows)
    alive = row_ids % ROWS_DEV < per_row
    normed = rms_normed(hidden, norm_gain)
    conv_input = jnp.dot(normed, in_weight[:, 0, :], preferred_element_type=jnp.float32).astype(jnp.bfloat16)
    gate_branch = jnp.dot(normed, in_weight[:, 1, :], preferred_element_type=jnp.float32)
    window = jnp.concatenate([conv_state, conv_input[:, None, :]], axis=1)
    convolved = lax.optimization_barrier(jnp.sum(window.astype(jnp.float32) * conv_weight[None], axis=1)) + conv_offset
    mixed_x = jax.nn.silu(convolved).astype(jnp.bfloat16)
    low_rank = jnp.dot(mixed_x, coef_weight, preferred_element_type=jnp.float32)
    step_low = low_rank[:, :DTR].astype(jnp.bfloat16)
    in_coef = low_rank[:, DTR:DTR + NSTATE]
    out_coef = low_rank[:, DTR + NSTATE:]
    step_size = jax.nn.softplus(jnp.dot(step_low, step_weight, preferred_element_type=jnp.float32) + step_bias)
    x_wide = mixed_x.astype(jnp.float32)
    decays = jnp.exp(-step_size[:, None, :] * jnp.exp(log_rates)[None])
    old_state = ssm_state.astype(jnp.float32)
    updated = decays * old_state + step_size[:, None, :] * in_coef[:, :, None] * x_wide[:, None, :]
    readout = lax.optimization_barrier(jnp.sum(out_coef[:, :, None] * updated, axis=1)) + skip_gain * x_wide
    gated_out = jnp.where(alive[:, None], readout * jax.nn.silu(gate_branch), 0.0).astype(jnp.bfloat16)
    mixer_term = jnp.dot(gated_out, out_weight, preferred_element_type=jnp.float32)
    mixed = (hidden.astype(jnp.float32) + mixer_term).astype(jnp.bfloat16)
    new_state = jnp.where(alive[:, None, None], updated, old_state).astype(jnp.bfloat16)
    new_conv = jnp.where(alive[:, None, None], window[:, 1:], conv_state)
    return (mixed, new_state, new_conv)
```

```python
import functools

import jax
import jax.numpy as jnp
from jax import lax
from jax.experimental import pallas as pl
from jax.experimental.pallas import tpu as pltpu
from jax.sharding import PartitionSpec as P

NSTATE = 16
DTR = 512
LIVE_MAX = 3
LANES = 128
F32 = jnp.float32
BF16 = jnp.bfloat16
MESH = pl.DeviceIdType.MESH
KSPLIT = 8


def iota(shape, dim):
    return lax.broadcasted_iota(jnp.int32, shape, dim)


def dot(a, b):
    return jnp.dot(a, b, preferred_element_type=F32)


def kernel(
    n, lb,
    hidden, gain, convw, convo, sbias, lograte, skip, live,
    w_hbm, coef_hbm, stepw_hbm, outw_hbm, ssm_hbm, conv_hbm,
    mixed, state_out, conv_out,
    wv, coefv, stepv, outv, ssmv, convv, newconv,
    xs, xg, xf, acc, mx, sgate, lowp, lowr, lowg, inb, outb, step, ro, erate,
    pf, r1, k1, s2, r2, s3, r3, fin,
    wsem, lsem, osem, a_s, a_r, b_s, b_r, c_s, c_r, d_s, d_r, e_s, e_r, f_s, f_r, g_s, g_r, h_s, h_r,
):
    me = lax.axis_index("weight")
    core = me % 2
    y = (me // 2) % 2
    z = me // 4
    outer = n // 4
    depth = hidden.shape[1]
    rows_dev = hidden.shape[0]
    ch = depth // LANES
    blk = LIVE_MAX * ch
    rows = LIVE_MAX * n
    allrows = rows_dev * n
    tiles = wv.shape[0]
    chan = tiles * LANES
    kstep = depth // KSPLIT
    chunks = (DTR + 2 * NSTATE + LANES - 1) // LANES
    wide = DTR + 2 * NSTATE

    def at(zz, yy, cc):
        return zz * 4 + yy * 2 + cc

    def rdma(src, dst, send, recv, dev):
        return pltpu.make_async_remote_copy(
            src_ref=src, dst_ref=dst, send_sem=send, recv_sem=recv,
            device_id={"weight": dev}, device_id_type=MESH,
        )

    wcopies = []
    for s in range(KSPLIT):
        for j in range(tiles):
            cp = pltpu.make_async_copy(
                w_hbm.at[pl.ds(s * kstep, kstep), j], wv.at[j, pl.ds(s * kstep, kstep)], wsem.at[s, j]
            )
            cp.start()
            wcopies.append(cp)
    conv_cp = pltpu.make_async_copy(conv_hbm, convv, lsem.at[0])
    coef_cp = pltpu.make_async_copy(coef_hbm, coefv.at[pl.ds(0, wide)], lsem.at[1])
    step_cp = pltpu.make_async_copy(stepw_hbm, stepv, lsem.at[2])
    ssm_cp = pltpu.make_async_copy(ssm_hbm, ssmv, lsem.at[3])
    out_cp = pltpu.make_async_copy(outw_hbm, outv, lsem.at[4])
    for cp in (conv_cp, coef_cp, step_cp, ssm_cp, out_cp):
        cp.start()

    barrier = pltpu.get_barrier_semaphore()
    for k in range(1, n):
        pl.semaphore_signal(barrier, inc=1, device_id={"weight": (me + k) % n}, device_id_type=MESH)

    h = hidden[...].astype(F32)
    factor = lax.rsqrt(jnp.mean(h * h, axis=-1, keepdims=True) + 1e-05)
    nm = h * factor * gain[...]
    for c in range(ch):
        xs[pl.ds(c, rows_dev, stride=ch), :] = nm[:, c * LANES : (c + 1) * LANES]
    xg[me] = xs[pl.ds(0, blk), :].astype(BF16)
    coefv[pl.ds(wide, chunks * LANES - wide), :] = jnp.zeros((chunks * LANES - wide, chan), BF16)
    pl.semaphore_wait(barrier, n - 1)

    def widen(b):
        xf[pl.ds(pl.multiple_of(b * blk, 8), blk), :] = xg[b].astype(F32)

    sends = []
    for k in range(1, outer):
        cp = rdma(xg.at[me], xg.at[me], a_s.at[k], a_r.at[k], at((z + k) % outer, y, core))
        cp.start()
        sends.append(cp)
    ypeer = at(z, 1 - y, core)
    cpeer = at(z, y, 1 - core)
    for k in range(outer):
        zz = (z + outer - k) % outer
        b = at(zz, y, core)
        if k:
            rdma(xg.at[b], xg.at[b], a_s.at[k], a_r.at[k], ypeer).wait_recv()
        cp = rdma(xg.at[b], xg.at[b], b_s.at[k], b_r.at[k], ypeer)
        cp.start()
        sends.append(cp)
        cp = rdma(xg.at[b], xg.at[b], c_s.at[k], c_r.at[k], cpeer)
        cp.start()
        sends.append(cp)
        widen(b)
    for k in range(outer):
        b = at((z + outer - k) % outer, 1 - y, core)
        rdma(xg.at[b], xg.at[b], b_s.at[k], b_r.at[k], ypeer).wait_recv()
        cp = rdma(xg.at[b], xg.at[b], c_s.at[outer + k], c_r.at[outer + k], cpeer)
        cp.start()
        sends.append(cp)
        widen(b)
    for k in range(2 * outer):
        zz = (z + 2 * outer - k) % outer
        b = at(zz, y if k < outer else 1 - y, 1 - core)
        rdma(xg.at[b], xg.at[b], c_s.at[k], c_r.at[k], cpeer).wait_recv()
        widen(b)

    lane = iota((LANES, 4 * LANES), 1)
    spread = jnp.where(
        (lane % (2 * LANES) == 2 * iota((LANES, 4 * LANES), 0) + lane // (2 * LANES)), 1.0, 0.0
    ).astype(BF16)
    acc[...] = jnp.zeros_like(acc)
    for cp in wcopies:
        cp.wait()
    per = kstep // LANES

    @pl.loop(0, KSPLIT)
    def _(s):
        tops, lows = [], []
        for i in range(per):
            xc = xf[pl.ds(s * per + i, rows, stride=ch), :].astype(BF16)
            e = dot(xc, spread).astype(BF16)
            tops.append(e[:, : 2 * LANES])
            lows.append(e[:, 2 * LANES :])
        lhs = jnp.concatenate(
            [jnp.concatenate(tops, axis=1), jnp.concatenate(lows, axis=1)], axis=0
        )
        rhs = jnp.concatenate(
            [
                wv.at[j].reshape(2 * depth, LANES)[pl.ds(pl.multiple_of(s * 2 * kstep, 16), 2 * kstep), :]
                for j in range(tiles)
            ],
            axis=1,
        )
        acc[...] += dot(lhs, rhs)

    conv_cp.wait()
    ci = acc[pl.ds(0, rows), :].astype(BF16)
    cif = ci.astype(F32)
    r_at, c_at = iota((rows, allrows), 0), iota((rows, allrows), 1)
    pick = jnp.where(
        (c_at % rows_dev < LIVE_MAX) & (c_at // rows_dev * LIVE_MAX + c_at % rows_dev == r_at), 1.0, 0.0
    ).astype(BF16)
    total = cif * convw[pl.ds(3, 1), :] + convo[...]
    for t in range(3):
        total = total + dot(pick, convv[t]) * convw[pl.ds(t, 1), :]
    x = (total / (1.0 + jnp.exp(-total))).astype(BF16)
    mx[...] = x.astype(F32)

    coef_cp.wait()
    part = lax.dot_general(x, coefv[...], (((1,), (1,)), ((), ())), preferred_element_type=F32)
    for c in range(chunks):
        lowp[pl.ds(c * rows, rows), :] = part[:, c * LANES : (c + 1) * LANES]
    if n * lb > chunks * rows:
        lowp[pl.ds(chunks * rows, n * lb - chunks * rows), :] = jnp.zeros(
            (n * lb - chunks * rows, LANES), F32
        )

    def low_at(ref, d):
        return ref.at[pl.ds(pl.multiple_of(d * lb, 8), lb)]

    for k in range(1, n):
        d = (me + k) % n
        cp = rdma(low_at(lowp, d), lowr.at[k], d_s.at[k], d_r.at[k], d)
        cp.start()
        sends.append(cp)

    g = acc[pl.ds(rows, rows), :]
    sgate[...] = g / (1.0 + jnp.exp(-g))
    erate[...] = jnp.exp(lograte[...])
    row4 = iota((allrows, chan), 0)
    count4 = jnp.zeros((allrows, chan), jnp.int32)
    for m in range(n):
        count4 = jnp.where(row4 // rows_dev == m, live[m], count4)
    alive4 = row4 % rows_dev < count4
    t_at, s_at = iota((allrows, rows), 1), iota((allrows, rows), 0)
    put = jnp.where(
        (s_at % rows_dev < LIVE_MAX) & (s_at // rows_dev * LIVE_MAX + s_at % rows_dev == t_at), 1.0, 0.0
    ).astype(BF16)
    for t in range(3):
        new = convv[t + 1].astype(F32) if t < 2 else dot(put, ci)
        newconv[t] = jnp.where(alive4, new, convv[t].astype(F32)).astype(BF16)
    conv_done = pltpu.make_async_copy(newconv, conv_out, osem.at[0])
    conv_done.start()

    own = low_at(lowp, me)[...]
    for k in range(1, n):
        rdma(lowr.at[k], lowr.at[k], d_s.at[k], d_r.at[k], ypeer).wait_recv()
        own = own + lowr[k]
    low_at(lowg, me)[...] = own
    for k in range(1, n):
        d = (me + k) % n
        cp = rdma(low_at(lowg, me), low_at(lowg, me), e_s.at[k], e_r.at[k], d)
        cp.start()
        sends.append(cp)
    for k in range(1, n):
        src = low_at(lowg, (me + n - k) % n)
        rdma(src, src, e_s.at[k], e_r.at[k], ypeer).wait_recv()

    step_cp.wait()
    low = jnp.concatenate(
        [lowg[pl.ds(c * rows, rows), :] for c in range(DTR // LANES)], axis=1
    ).astype(BF16)
    v = dot(low, stepv[...]) + sbias[...]
    step[...] = jnp.maximum(v, 0.0) + jnp.log1p(jnp.exp(-jnp.abs(v)))
    coefs = lowg[pl.ds(DTR // LANES * rows, rows), :]
    for q in range(NSTATE):
        inb[pl.ds(q, rows, stride=NSTATE), :] = jnp.broadcast_to(coefs[:, q : q + 1], (rows, LANES))
        outb[pl.ds(q, rows, stride=NSTATE), :] = jnp.broadcast_to(
            coefs[:, NSTATE + q : NSTATE + q + 1], (rows, LANES)
        )
    ssm_cp.wait()

    @pl.loop(0, n)
    def _(m):
        count = live[m]
        for j in range(LIVE_MAX):
            r = m * LIVE_MAX + j
            old = ssmv[m * rows_dev + j].astype(F32)
            st = step[pl.ds(r, 1), :]
            xr = mx[pl.ds(r, 1), :]
            at_r = pl.ds(pl.multiple_of(r * NSTATE, NSTATE), NSTATE)
            inc = jnp.concatenate([inb[at_r, :]] * tiles, axis=1)
            outc = jnp.concatenate([outb[at_r, :]] * tiles, axis=1)
            upd = jnp.exp(-st * erate[...]) * old + st * inc * xr
            ro[pl.ds(r, 1), :] = jnp.sum(outc * upd, axis=0, keepdims=True)
            keep = jnp.full(old.shape, count, jnp.int32) > j
            ssmv[m * rows_dev + j] = jnp.where(keep, upd, old).astype(BF16)

    state_done = pltpu.make_async_copy(ssmv, state_out, osem.at[1])
    state_done.start()

    row3 = iota((rows, chan), 0)
    count3 = jnp.zeros((rows, chan), jnp.int32)
    for m in range(n):
        count3 = jnp.where(row3 // LIVE_MAX == m, live[m], count3)
    read = (ro[...] + skip[...] * mx[...]) * sgate[...]
    gated = jnp.where(row3 % LIVE_MAX < count3, read, 0.0).astype(BF16)

    out_cp.wait()
    ntile = 8

    @pl.loop(0, ch // ntile)
    def _(t):
        p = dot(gated, outv[:, pl.ds(pl.multiple_of(t * ntile * LANES, LANES), ntile * LANES)])
        for i in range(ntile):
            pf[pl.ds(t * ntile + i, rows, stride=ch), :] = p[:, i * LANES : (i + 1) * LANES]

    def pf_at(d):
        return pf.at[pl.ds(pl.multiple_of(d * blk, 8), blk)]

    order = [(k, yy) for yy in (0, 1) for k in range(outer)]
    for i, (k, flip) in enumerate(order):
        zz = (z + k) % outer
        yy = 1 - y if flip == 0 else y
        cp = rdma(pf_at(at(zz, yy, 1 - core)), r1.at[i], f_s.at[i], f_r.at[i], cpeer)
        cp.start()
        sends.append(cp)
    for i, (k, flip) in enumerate(order):
        zz = (z + k) % outer
        yy = 1 - y if flip == 0 else y
        rdma(r1.at[i], r1.at[i], f_s.at[i], f_r.at[i], cpeer).wait_recv()
        both = pf_at(at(zz, yy, core))[...] + r1[i]
        if flip == 0:
            s2[k] = both.astype(BF16)
            cp = rdma(s2.at[k], r2.at[k], g_s.at[k], g_r.at[k], ypeer)
            cp.start()
            sends.append(cp)
        else:
            k1[k] = both
    for k in list(range(1, outer)) + [0]:
        rdma(r2.at[k], r2.at[k], g_s.at[k], g_r.at[k], ypeer).wait_recv()
        both = k1[k] + r2[k].astype(F32)
        if k:
            s3[k] = both.astype(BF16)
            cp = rdma(s3.at[k], r3.at[k], h_s.at[k], h_r.at[k], at((z + k) % outer, y, core))
            cp.start()
            sends.append(cp)
    for k in range(1, outer):
        rdma(r3.at[k], r3.at[k], h_s.at[k], h_r.at[k], ypeer).wait_recv()
        both = both + r3[k].astype(F32)
    fin[pl.ds(0, blk), :] = both
    fin[pl.ds(blk, ch * rows_dev - blk), :] = jnp.zeros((ch * rows_dev - blk, LANES), F32)
    for c in range(ch):
        cols = slice(c * LANES, (c + 1) * LANES)
        mixed[:, cols] = (hidden[:, cols].astype(F32) + fin[pl.ds(c, rows_dev, stride=ch), :]).astype(BF16)
    for cp in sends:
        cp.wait_send()
    conv_done.wait()
    state_done.wait()


def body(
    hidden, norm_gain, in_weight, conv_weight, conv_offset, coef_weight, step_weight,
    step_bias, log_rates, skip_gain, out_weight, ssm_state, conv_state, live_counts,
):
    n = lax.axis_size("weight")
    rows_dev, depth = hidden.shape
    chan = in_weight.shape[2]
    tiles = chan // LANES
    ch = depth // LANES
    rows = LIVE_MAX * n
    allrows = rows_dev * n
    blk = LIVE_MAX * ch
    outer = n // 4
    chunks = (DTR + 2 * NSTATE + LANES - 1) // LANES
    lb = -(-(chunks * rows) // (8 * n)) * 8
    weight = in_weight.reshape(depth, 2, tiles, LANES).transpose(0, 2, 1, 3)
    vmem = pl.BlockSpec(memory_space=pltpu.VMEM)
    smem = pl.BlockSpec(memory_space=pltpu.SMEM)
    hbm = pl.BlockSpec(memory_space=pl.ANY)
    dma = pltpu.SemaphoreType.DMA
    V = pltpu.VMEM
    mixed, new_state, new_conv = pl.pallas_call(
        functools.partial(kernel, n, lb),
        out_shape=(
            jax.ShapeDtypeStruct(hidden.shape, BF16),
            jax.ShapeDtypeStruct(ssm_state.shape, BF16),
            jax.ShapeDtypeStruct((3, allrows, chan), BF16),
        ),
        in_specs=[vmem] * 7 + [smem] + [hbm] * 6,
        out_specs=(vmem, hbm, hbm),
        scratch_shapes=[
            V((tiles, depth, 2, LANES), BF16),
            V((chunks * LANES, chan), BF16),
            V(step_weight.shape, BF16),
            V(out_weight.shape, BF16),
            V(ssm_state.shape, BF16),
            V((3, allrows, chan), BF16),
            V((3, allrows, chan), BF16),
            V((rows_dev * ch, LANES), F32),
            V((n, blk, LANES), BF16),
            V((n * blk, LANES), F32),
            V((2 * rows, chan), F32),
            V((rows, chan), F32),
            V((rows, chan), F32),
            V((n * lb, LANES), F32),
            V((n, lb, LANES), F32),
            V((n * lb, LANES), F32),
            V((rows * NSTATE, LANES), F32),
            V((rows * NSTATE, LANES), F32),
            V((rows, chan), F32),
            V((rows, chan), F32),
            V((NSTATE, chan), F32),
            V((n * blk, LANES), F32),
            V((2 * outer, blk, LANES), F32),
            V((outer, blk, LANES), F32),
            V((outer, blk, LANES), BF16),
            V((outer, blk, LANES), BF16),
            V((outer, blk, LANES), BF16),
            V((outer, blk, LANES), BF16),
            V((rows_dev * ch, LANES), F32),
            dma((KSPLIT, tiles)),
            dma((5,)),
            dma((2,)),
            dma((outer,)), dma((outer,)),
            dma((outer,)), dma((outer,)),
            dma((2 * outer,)), dma((2 * outer,)),
            dma((n,)), dma((n,)),
            dma((n,)), dma((n,)),
            dma((2 * outer,)), dma((2 * outer,)),
            dma((outer,)), dma((outer,)),
            dma((outer,)), dma((outer,)),
        ],
        compiler_params=pltpu.CompilerParams(
            collective_id=0, has_side_effects=True, vmem_limit_bytes=58 * 1024 * 1024
        ),
        name="mixer",
    )(
        hidden, norm_gain[None], conv_weight, conv_offset[None], step_bias[None], log_rates,
        skip_gain[None], live_counts,
        weight, coef_weight.T, step_weight, out_weight, ssm_state, conv_state.transpose(1, 0, 2),
    )
    return mixed, new_state, new_conv.transpose(1, 0, 2)


def solution(mesh):
    in_specs = (
        P(("groups", "weight"), None),
        P(),
        P(None, None, "weight"),
        P(None, "weight"),
        P("weight"),
        P("weight", None),
        P(None, "weight"),
        P("weight"),
        P(None, "weight"),
        P("weight"),
        P("weight", None),
        P("groups", None, "weight"),
        P("groups", None, "weight"),
        P("groups"),
    )
    out_specs = (
        P(("groups", "weight"), None),
        P("groups", None, "weight"),
        P("groups", None, "weight"),
    )
    return jax.shard_map(body, mesh=mesh, in_specs=in_specs, out_specs=out_specs, check_vma=False)
```

```python
import functools

import jax
import jax.numpy as jnp
from jax import lax
from jax.experimental import pallas as pl
from jax.experimental.pallas import tpu as pltpu
from jax.sharding import PartitionSpec as P

NSTATE = 16
DTR = 512
LIVE_MAX = 3
LANES = 128
F32 = jnp.float32
BF16 = jnp.bfloat16
MESH = pl.DeviceIdType.MESH
KSPLIT = 8
PARTS = 4


def iota(shape, dim):
    return lax.broadcasted_iota(jnp.int32, shape, dim)


def dot(a, b):
    return jnp.dot(a, b, preferred_element_type=F32)


def kernel(
    n, lb,
    hidden, gain, convw, convo, sbias, lograte, skip, live,
    w_hbm, coef_hbm, stepw_hbm, outw_hbm, ssm_hbm, conv_hbm,
    mixed, state_out, conv_out,
    wv, coefv, stepv, outv, ssmv, convv, newconv,
    xs, xg, xf, acc, mx, sgate, lowp, lowr, lowg, inb, outb, step, ro, erate,
    pf, r1, k1, s2, r2, s3, r3, fin,
    wsem, lsem, osem, a_s, a_r, b_s, b_r, c_s, c_r, d_s, d_r, e_s, e_r, f_s, f_r, g_s, g_r, h_s, h_r,
):
    me = lax.axis_index("weight")
    core = me % 2
    y = (me // 2) % 2
    z = me // 4
    outer = n // 4
    depth = hidden.shape[1]
    rows_dev = hidden.shape[0]
    ch = depth // LANES
    blk = LIVE_MAX * ch
    rows = LIVE_MAX * n
    allrows = rows_dev * n
    tiles = wv.shape[0]
    chan = tiles * LANES
    kstep = depth // KSPLIT
    chq = ch // PARTS
    bq = LIVE_MAX * chq
    span = n * bq
    chunks = (DTR + 2 * NSTATE + LANES - 1) // LANES
    wide = DTR + 2 * NSTATE

    def at(zz, yy, cc):
        return zz * 4 + yy * 2 + cc

    def rdma(src, dst, send, recv, dev):
        return pltpu.make_async_remote_copy(
            src_ref=src, dst_ref=dst, send_sem=send, recv_sem=recv,
            device_id={"weight": dev}, device_id_type=MESH,
        )

    wcopies = []
    for s in range(KSPLIT):
        for j in range(tiles):
            cp = pltpu.make_async_copy(
                w_hbm.at[pl.ds(s * kstep, kstep), j], wv.at[j, pl.ds(s * kstep, kstep)], wsem.at[s, j]
            )
            cp.start()
            wcopies.append(cp)
    conv_cp = pltpu.make_async_copy(conv_hbm, convv, lsem.at[0])
    coef_cp = pltpu.make_async_copy(coef_hbm, coefv.at[pl.ds(0, wide)], lsem.at[1])
    step_cp = pltpu.make_async_copy(stepw_hbm, stepv, lsem.at[2])
    ssm_cp = pltpu.make_async_copy(ssm_hbm, ssmv, lsem.at[3])
    out_cp = pltpu.make_async_copy(outw_hbm, outv, lsem.at[4])
    for cp in (conv_cp, coef_cp, step_cp, ssm_cp, out_cp):
        cp.start()

    barrier = pltpu.get_barrier_semaphore()
    for k in range(1, n):
        pl.semaphore_signal(barrier, inc=1, device_id={"weight": (me + k) % n}, device_id_type=MESH)

    h = hidden[...].astype(F32)
    factor = lax.rsqrt(jnp.mean(h * h, axis=-1, keepdims=True) + 1e-05)
    nm = h * factor * gain[...]
    for c in range(ch):
        xs[pl.ds(c, rows_dev, stride=ch), :] = nm[:, c * LANES : (c + 1) * LANES]
    for q in range(PARTS):
        for j in range(LIVE_MAX):
            xg[q, me, pl.ds(j * chq, chq), :] = xs[pl.ds(j * ch + q * chq, chq), :].astype(BF16)
    coefv[pl.ds(wide, chunks * LANES - wide), :] = jnp.zeros((chunks * LANES - wide, chan), BF16)
    pl.semaphore_wait(barrier, n - 1)

    sends = []
    ypeer = at(z, 1 - y, core)
    cpeer = at(z, y, 1 - core)

    def near(k):
        low, high = z, outer - 1 - z
        least = jnp.minimum(low, high)
        both = (k + 1) // 2 * (1 if k % 2 else -1)
        one = (k - least) * jnp.where(high > low, 1, -1)
        return z + jnp.where(k <= 2 * least, both, one)

    places = [z] + [near(k) for k in range(1, outer)]

    def move(q, b, send, recv, slot, dev):
        return rdma(xg.at[q, b], xg.at[q, b], send.at[q, slot], recv.at[q, slot], dev)

    def go(cp):
        cp.start()
        sends.append(cp)

    for q in range(PARTS):
        for k in range(outer - 1, 0, -1):
            cp = rdma(xg.at[q, me], xg.at[q, me], a_s.at[q, k], a_r.at[q, z], at(places[k], y, core))
            go(cp)
        go(move(q, me, b_s, b_r, z, ypeer))
        go(move(q, me, c_s, c_r, 2 * z + y, cpeer))

    def forward_z(q):
        for k in range(1, outer):
            p = places[k]
            b = at(p, y, core)
            rdma(xg.at[q, b], xg.at[q, b], a_s.at[q, k], a_r.at[q, p], ypeer).wait_recv()
            go(move(q, b, b_s, b_r, p, ypeer))
            go(move(q, b, c_s, c_r, 2 * p + y, cpeer))

    def forward_y(q):
        for p in places:
            b = at(p, 1 - y, core)
            move(q, b, b_s, b_r, p, ypeer).wait_recv()
            go(move(q, b, c_s, c_r, 2 * p + 1 - y, cpeer))

    def arrived(q):
        for p in places:
            for yy in (y, 1 - y):
                move(q, at(p, yy, 1 - core), c_s, c_r, 2 * p + yy, cpeer).wait_recv()
        xf[pl.ds(q * span, span), :] = jnp.concatenate([xg[q, b] for b in range(n)], axis=0).astype(F32)

    lane = iota((LANES, 4 * LANES), 1)
    spread = jnp.where(
        (lane % (2 * LANES) == 2 * iota((LANES, 4 * LANES), 0) + lane // (2 * LANES)), 1.0, 0.0
    ).astype(BF16)
    per = kstep // LANES

    def project(s):
        first = s * per
        q, base = first // chq, first % chq
        x = jnp.concatenate(
            [xf[pl.ds(q * span + base + i, rows, stride=chq), :] for i in range(per)], axis=0
        ).astype(BF16)
        e = dot(x, spread).astype(BF16)
        lhs = jnp.concatenate(
            [
                jnp.concatenate(
                    [e[i * rows : (i + 1) * rows, h * 2 * LANES : (h + 1) * 2 * LANES] for i in range(per)],
                    axis=1,
                )
                for h in range(2)
            ],
            axis=0,
        )
        for j in range(tiles):
            wcopies[s * tiles + j].wait()
        rhs = jnp.concatenate(
            [wv.at[j].reshape(2 * depth, LANES)[pl.ds(s * 2 * kstep, 2 * kstep), :] for j in range(tiles)],
            axis=1,
        )
        if s == 0:
            acc[...] = dot(lhs, rhs)
        else:
            acc[...] += dot(lhs, rhs)

    forward_z(0)
    forward_y(0)
    for q in range(PARTS):
        if q + 1 < PARTS:
            forward_z(q + 1)
        arrived(q)
        for s in range(q * KSPLIT // PARTS, (q + 1) * KSPLIT // PARTS):
            project(s)
            if q + 1 < PARTS and s == q * KSPLIT // PARTS:
                forward_y(q + 1)

    conv_cp.wait()
    ci = acc[pl.ds(0, rows), :].astype(BF16)
    cif = ci.astype(F32)
    r_at, c_at = iota((rows, allrows), 0), iota((rows, allrows), 1)
    pick = jnp.where(
        (c_at % rows_dev < LIVE_MAX) & (c_at // rows_dev * LIVE_MAX + c_at % rows_dev == r_at), 1.0, 0.0
    ).astype(BF16)
    total = cif * convw[pl.ds(3, 1), :] + convo[...]
    for t in range(3):
        total = total + dot(pick, convv[t]) * convw[pl.ds(t, 1), :]
    x = (total / (1.0 + jnp.exp(-total))).astype(BF16)
    mx[...] = x.astype(F32)

    coef_cp.wait()
    part = lax.dot_general(x, coefv[...], (((1,), (1,)), ((), ())), preferred_element_type=F32)
    for c in range(chunks):
        lowp[pl.ds(c * rows, rows), :] = part[:, c * LANES : (c + 1) * LANES]
    if n * lb > chunks * rows:
        lowp[pl.ds(chunks * rows, n * lb - chunks * rows), :] = jnp.zeros(
            (n * lb - chunks * rows, LANES), F32
        )

    def low_at(ref, d):
        return ref.at[pl.ds(pl.multiple_of(d * lb, 8), lb)]

    for k in range(1, n):
        d = (me + k) % n
        cp = rdma(low_at(lowp, d), lowr.at[k], d_s.at[k], d_r.at[k], d)
        cp.start()
        sends.append(cp)

    g = acc[pl.ds(rows, rows), :]
    sgate[...] = g / (1.0 + jnp.exp(-g))
    erate[...] = jnp.exp(lograte[...])
    row4 = iota((allrows, chan), 0)
    count4 = jnp.zeros((allrows, chan), jnp.int32)
    for m in range(n):
        count4 = jnp.where(row4 // rows_dev == m, live[m], count4)
    alive4 = row4 % rows_dev < count4
    t_at, s_at = iota((allrows, rows), 1), iota((allrows, rows), 0)
    put = jnp.where(
        (s_at % rows_dev < LIVE_MAX) & (s_at // rows_dev * LIVE_MAX + s_at % rows_dev == t_at), 1.0, 0.0
    ).astype(BF16)
    for t in range(3):
        new = convv[t + 1].astype(F32) if t < 2 else dot(put, ci)
        newconv[t] = jnp.where(alive4, new, convv[t].astype(F32)).astype(BF16)
    conv_done = pltpu.make_async_copy(newconv, conv_out, osem.at[0])
    conv_done.start()

    own = low_at(lowp, me)[...]
    for k in range(1, n):
        rdma(lowr.at[k], lowr.at[k], d_s.at[k], d_r.at[k], ypeer).wait_recv()
        own = own + lowr[k]
    low_at(lowg, me)[...] = own
    for k in range(1, n):
        d = (me + k) % n
        cp = rdma(low_at(lowg, me), low_at(lowg, me), e_s.at[k], e_r.at[k], d)
        cp.start()
        sends.append(cp)
    for k in range(1, n):
        src = low_at(lowg, (me + n - k) % n)
        rdma(src, src, e_s.at[k], e_r.at[k], ypeer).wait_recv()

    step_cp.wait()
    low = jnp.concatenate(
        [lowg[pl.ds(c * rows, rows), :] for c in range(DTR // LANES)], axis=1
    ).astype(BF16)
    v = dot(low, stepv[...]) + sbias[...]
    step[...] = jnp.maximum(v, 0.0) + jnp.log1p(jnp.exp(-jnp.abs(v)))
    coefs = lowg[pl.ds(DTR // LANES * rows, rows), :]
    for q in range(NSTATE):
        inb[pl.ds(q, rows, stride=NSTATE), :] = jnp.broadcast_to(coefs[:, q : q + 1], (rows, LANES))
        outb[pl.ds(q, rows, stride=NSTATE), :] = jnp.broadcast_to(
            coefs[:, NSTATE + q : NSTATE + q + 1], (rows, LANES)
        )
    ssm_cp.wait()

    @pl.loop(0, n)
    def _(m):
        count = live[m]
        for j in range(LIVE_MAX):
            r = m * LIVE_MAX + j
            old = ssmv[m * rows_dev + j].astype(F32)
            st = step[pl.ds(r, 1), :]
            xr = mx[pl.ds(r, 1), :]
            at_r = pl.ds(pl.multiple_of(r * NSTATE, NSTATE), NSTATE)
            inc = jnp.concatenate([inb[at_r, :]] * tiles, axis=1)
            outc = jnp.concatenate([outb[at_r, :]] * tiles, axis=1)
            upd = jnp.exp(-st * erate[...]) * old + st * inc * xr
            ro[pl.ds(r, 1), :] = jnp.sum(outc * upd, axis=0, keepdims=True)
            keep = jnp.full(old.shape, count, jnp.int32) > j
            ssmv[m * rows_dev + j] = jnp.where(keep, upd, old).astype(BF16)

    state_done = pltpu.make_async_copy(ssmv, state_out, osem.at[1])
    state_done.start()

    row3 = iota((rows, chan), 0)
    count3 = jnp.zeros((rows, chan), jnp.int32)
    for m in range(n):
        count3 = jnp.where(row3 // LIVE_MAX == m, live[m], count3)
    read = (ro[...] + skip[...] * mx[...]) * sgate[...]
    gated = jnp.where(row3 % LIVE_MAX < count3, read, 0.0).astype(BF16)

    out_cp.wait()
    cols = chq * LANES

    def pf_at(h, d):
        return pf.at[pl.ds(pl.multiple_of(h * span + d * bq, 8), bq)]

    def stage1(h):
        p = dot(gated, outv[:, pl.ds(h * cols, cols)])
        for i in range(chq):
            pf[pl.ds(h * span + i, rows, stride=chq), :] = p[:, i * LANES : (i + 1) * LANES]
        for yy in (1 - y, y):
            for k in range(outer - 1, -1, -1):
                slot = 2 * places[k] + yy
                go(rdma(pf_at(h, at(places[k], yy, 1 - core)), r1.at[h, slot], f_s.at[h, slot], f_r.at[h, slot], cpeer))

    def paired(h, k, yy):
        slot = 2 * places[k] + yy
        rdma(r1.at[h, slot], r1.at[h, slot], f_s.at[h, slot], f_r.at[h, slot], cpeer).wait_recv()
        return pf_at(h, at(places[k], yy, core))[...] + r1[h, slot]

    def stage2(h):
        for k in range(outer - 1, -1, -1):
            p = places[k]
            s2[h, p] = paired(h, k, 1 - y).astype(BF16)
            go(rdma(s2.at[h, p], r2.at[h, p], g_s.at[h, p], g_r.at[h, p], ypeer))

    def stage3(h):
        for k in range(outer - 1, -1, -1):
            p = places[k]
            both = paired(h, k, y)
            rdma(r2.at[h, p], r2.at[h, p], g_s.at[h, p], g_r.at[h, p], ypeer).wait_recv()
            both = both + r2[h, p].astype(F32)
            if k:
                s3[h, p] = both.astype(BF16)
                go(rdma(s3.at[h, p], r3.at[h, z], h_s.at[h, p], h_r.at[h, z], at(p, y, core)))
            else:
                k1[h] = both

    def stage4(h):
        both = k1[h]
        for k in range(1, outer):
            p = places[k]
            rdma(r3.at[h, p], r3.at[h, p], h_s.at[h, p], h_r.at[h, p], ypeer).wait_recv()
            both = both + r3[h, p].astype(F32)
        for j in range(LIVE_MAX):
            fin[pl.ds(j * ch + h * chq, chq), :] = both[j * chq : (j + 1) * chq]

    for t in range(PARTS + 3):
        for late, stage in enumerate((stage1, stage2, stage3, stage4)):
            if 0 <= t - late < PARTS:
                stage(t - late)
    fin[pl.ds(blk, ch * rows_dev - blk), :] = jnp.zeros((ch * rows_dev - blk, LANES), F32)
    for c in range(ch):
        cols = slice(c * LANES, (c + 1) * LANES)
        mixed[:, cols] = (hidden[:, cols].astype(F32) + fin[pl.ds(c, rows_dev, stride=ch), :]).astype(BF16)
    for cp in sends:
        cp.wait_send()
    conv_done.wait()
    state_done.wait()


def hand_out(mixed, state, conv, mixed_out, state_out, conv_out, mixed_v, state_v, conv_v, sem_in, sem_out):
    half = state.shape[0] // 2
    trips = [
        (state.at[pl.ds(0, half)], state_v.at[pl.ds(0, half)], state_out.at[pl.ds(0, half)]),
        (state.at[pl.ds(half, half)], state_v.at[pl.ds(half, half)], state_out.at[pl.ds(half, half)]),
        (conv, conv_v, conv_out),
        (mixed, mixed_v, mixed_out),
    ]
    ins = [pltpu.make_async_copy(a, v, sem_in.at[i]) for i, (a, v, _) in enumerate(trips)]
    outs = [pltpu.make_async_copy(v, o, sem_out.at[i]) for i, (_, v, o) in enumerate(trips)]
    for cp in ins:
        cp.start()
    for first, second in zip(ins, outs):
        first.wait()
        second.start()
    for cp in outs:
        cp.wait()


def body(
    hidden, norm_gain, in_weight, conv_weight, conv_offset, coef_weight, step_weight,
    step_bias, log_rates, skip_gain, out_weight, ssm_state, conv_state, live_counts,
):
    n = lax.axis_size("weight")
    rows_dev, depth = hidden.shape
    chan = in_weight.shape[2]
    tiles = chan // LANES
    ch = depth // LANES
    rows = LIVE_MAX * n
    allrows = rows_dev * n
    blk = LIVE_MAX * ch
    outer = n // 4
    bq = blk // PARTS
    chunks = (DTR + 2 * NSTATE + LANES - 1) // LANES
    lb = -(-(chunks * rows) // (8 * n)) * 8
    weight = in_weight.reshape(depth, 2, tiles, LANES).transpose(0, 2, 1, 3)
    vmem = pl.BlockSpec(memory_space=pltpu.VMEM)
    smem = pl.BlockSpec(memory_space=pltpu.SMEM)
    hbm = pl.BlockSpec(memory_space=pl.ANY)
    dma = pltpu.SemaphoreType.DMA
    V = pltpu.VMEM
    mixed, new_state, new_conv = pl.pallas_call(
        functools.partial(kernel, n, lb),
        out_shape=(
            jax.ShapeDtypeStruct(hidden.shape, BF16),
            jax.ShapeDtypeStruct(ssm_state.shape, BF16),
            jax.ShapeDtypeStruct((3, allrows, chan), BF16),
        ),
        in_specs=[vmem] * 7 + [smem] + [hbm] * 6,
        out_specs=(vmem, hbm, hbm),
        scratch_shapes=[
            V((tiles, depth, 2, LANES), BF16),
            V((chunks * LANES, chan), BF16),
            V(step_weight.shape, BF16),
            V(out_weight.shape, BF16),
            V(ssm_state.shape, BF16),
            V((3, allrows, chan), BF16),
            V((3, allrows, chan), BF16),
            V((rows_dev * ch, LANES), F32),
            V((PARTS, n, bq, LANES), BF16),
            V((n * blk, LANES), F32),
            V((2 * rows, chan), F32),
            V((rows, chan), F32),
            V((rows, chan), F32),
            V((n * lb, LANES), F32),
            V((n, lb, LANES), F32),
            V((n * lb, LANES), F32),
            V((rows * NSTATE, LANES), F32),
            V((rows * NSTATE, LANES), F32),
            V((rows, chan), F32),
            V((rows, chan), F32),
            V((NSTATE, chan), F32),
            V((n * blk, LANES), F32),
            V((PARTS, 2 * outer, bq, LANES), F32),
            V((PARTS, bq, LANES), F32),
            V((PARTS, outer, bq, LANES), BF16),
            V((PARTS, outer, bq, LANES), BF16),
            V((PARTS, outer, bq, LANES), BF16),
            V((PARTS, outer, bq, LANES), BF16),
            V((rows_dev * ch, LANES), F32),
            dma((KSPLIT, tiles)),
            dma((5,)),
            dma((2,)),
            dma((PARTS, outer)), dma((PARTS, outer)),
            dma((PARTS, outer)), dma((PARTS, outer)),
            dma((PARTS, 2 * outer)), dma((PARTS, 2 * outer)),
            dma((n,)), dma((n,)),
            dma((n,)), dma((n,)),
            dma((PARTS, 2 * outer)), dma((PARTS, 2 * outer)),
            dma((PARTS, outer)), dma((PARTS, outer)),
            dma((PARTS, outer)), dma((PARTS, outer)),
        ],
        compiler_params=pltpu.CompilerParams(
            collective_id=0, has_side_effects=True, vmem_limit_bytes=58 * 1024 * 1024
        ),
        name="mixer",
    )(
        hidden, norm_gain[None], conv_weight, conv_offset[None], step_bias[None], log_rates,
        skip_gain[None], live_counts,
        weight, coef_weight.T, step_weight, out_weight, ssm_state, conv_state.transpose(1, 0, 2),
    )
    mixed, new_state, new_conv = pl.pallas_call(
        hand_out,
        out_shape=tuple(jax.ShapeDtypeStruct(a.shape, a.dtype) for a in (mixed, new_state, new_conv)),
        in_specs=[hbm] * 3,
        out_specs=(hbm,) * 3,
        scratch_shapes=[V(a.shape, a.dtype) for a in (mixed, new_state, new_conv)] + [dma((4,)), dma((4,))],
        name="hand_out",
    )(mixed, new_state, new_conv)
    return mixed, new_state, new_conv.transpose(1, 0, 2)


def solution(mesh):
    in_specs = (
        P(("groups", "weight"), None),
        P(),
        P(None, None, "weight"),
        P(None, "weight"),
        P("weight"),
        P("weight", None),
        P(None, "weight"),
        P("weight"),
        P(None, "weight"),
        P("weight"),
        P("weight", None),
        P("groups", None, "weight"),
        P("groups", None, "weight"),
        P("groups"),
    )
    out_specs = (
        P(("groups", "weight"), None),
        P("groups", None, "weight"),
        P("groups", None, "weight"),
    )
    return jax.shard_map(body, mesh=mesh, in_specs=in_specs, out_specs=out_specs, check_vma=False)
```
